32 devices in a mesh: row: 4 (over y, x), col: 8 (over z, core).
Axes of the slice: x: 2, y: 2, z: 4, core: 2. Of those that a mesh axis runs over, the one named last changes fastest.
Arguments:
- factor: bfloat16 [7168, 7168], P('row', 'col'), may hold values from -2 to 2, as said below
- gradient: float32 [7168, 512], P(('row', 'col')), may hold values from -6 to 6
- starts: int32 [4], replicated, may hold values from 0 to 3, each once
Outputs:
- solved: float32 [7168, 512], P(('row', 'col'))
The draws below stay inside these ranges and needn't reach their ends.
Inputs may be any that keep to these rules, and one draw needn't show every extreme that they name: `factor`: tiles above the block diagonal are zero, and every diagonal tile is upper triangular. `starts`: every block column is the start of exactly one panel.
All inputs are finite; a program needn't handle non-finite values.
Results may differ from the reference program's by a relative error of at most 0.0046.
Values may be sent and summed in bfloat16 or wider, within the bound.
No kernel may reach another device: no remote copies, remote signals or barrier semaphores. Data moves between devices by JAX's collectives and lax.ppermute only.
A program may use at most 64 MiB of HBM per device.

```python
import math
import jax
import jax.numpy as jnp
from jax import lax

TILE = 1792
PANEL = 128
TICKS = 6
BLOCKS = 4
ORDER = 7168


def draw_factor(key, part):
    noise_key, diag_key = jax.random.split(jax.random.fold_in(key, 17))
    noise_draw = jax.random.normal(noise_key, (ORDER, ORDER), jnp.float32)
    scales = jnp.exp(jax.random.uniform(diag_key, (ORDER,), jnp.float32, math.log(0.5), math.log(2.0)))
    row_ids = lax.broadcasted_iota(jnp.int32, (ORDER, ORDER), 0)
    col_ids = lax.broadcasted_iota(jnp.int32, (ORDER, ORDER), 1)
    below_blocks = row_ids // TILE > col_ids // TILE
    inside = (row_ids // TILE == col_ids // TILE) & (row_ids < col_ids)
    scaled = noise_draw * (0.5 / math.sqrt(TILE))
    values = jnp.where(below_blocks | inside, scaled, 0.0)
    values = values + jnp.where(row_ids == col_ids, scales[None, :], 0.0)
    return values.astype(jnp.bfloat16)


def steps_of(stream_key, extent, cuts, least, top_value):
    loudness = 1.0
    for position, parts in cuts:
        draws = jax.random.uniform(jax.random.fold_in(jax.random.fold_in(stream_key, 6), position), (parts,), jnp.float32, least / len(cuts), top_value / len(cuts))
        loudness = loudness * jnp.repeat(jnp.exp(draws), extent[position] // parts).reshape((-1,) + (1,) * (len(extent) - 1 - position))
    return loudness


def normal_values(rng, extent, width, most, cuts=(), held_as=jnp.bfloat16):
    values = jax.random.normal(rng, extent, jnp.float32) * width
    if len(cuts) > 0:
        values = steps_of(rng, extent, cuts, -0.22, 0.18) * values
    return jnp.clip(values, min=-most, max=most).astype(held_as)


def setup_inputs(seed: int = 0) -> dict:
    keys = jax.random.split(jax.random.key(seed), 4)
    factor = draw_factor(jax.random.fold_in(keys[3], 71), 0)
    gradient = normal_values(keys[1], (ORDER, BLOCKS * PANEL), 1.0, 6.0, ((0, 32),), jnp.float32)
    starts = jax.random.permutation(keys[2], BLOCKS).astype(jnp.int32)
    return dict(factor=factor, gradient=gradient, starts=starts)


def reference(factor, gradient, starts):
    panels = gradient.reshape(ORDER, BLOCKS, PANEL).transpose(1, 0, 2)
    row_ids = jnp.arange(ORDER, dtype=jnp.int32)[:, None]

    def solve_panel(inputs):
        residual, start = inputs
        for tick_idx in range(TICKS):
            block_idx = start + tick_idx
            valid = block_idx < BLOCKS
            clamped = jnp.minimum(block_idx, BLOCKS - 1).astype(jnp.int32)
            begin = (clamped * TILE).astype(jnp.int32)
            column = lax.dynamic_slice_in_dim(factor, begin, TILE, 1)
            diag_tile = lax.dynamic_slice_in_dim(column, begin, TILE, 0)
            current = lax.dynamic_slice_in_dim(residual, begin, TILE, 0).astype(jnp.bfloat16)
            solution = jnp.dot(diag_tile.T, current, preferred_element_type=jnp.float32)
            update = jnp.dot(column, solution.astype(jnp.bfloat16), preferred_element_type=jnp.float32)
            below_rows = row_ids >= begin + TILE
            residual = jnp.where(valid & below_rows, residual - update, residual)
            written = lax.dynamic_update_slice_in_dim(residual, solution, begin, 0)
            residual = jnp.where(valid, written, residual)
        return residual

    result = lax.map(solve_panel, (panels, starts))
    return result.transpose(1, 0, 2).reshape(ORDER, BLOCKS * PANEL)
```

```python
import jax
import jax.numpy as jnp
from jax import lax
from jax.experimental import pallas as pl
from jax.experimental.pallas import tpu as pltpu
from jax.sharding import PartitionSpec as P

TICKS = 6
F32 = jnp.float32
BF16 = jnp.bfloat16
VM = pl.BlockSpec(memory_space=pltpu.VMEM)
SM = pl.BlockSpec(memory_space=pltpu.SMEM)


def call(kernel, outs, args, specs, scratch=(), flops=0, name=None):
    n_bytes = sum(o.size * o.dtype.itemsize for o in outs)
    return pl.pallas_call(
        kernel,
        out_shape=outs,
        in_specs=specs,
        out_specs=[VM] * len(outs),
        scratch_shapes=list(scratch),
        compiler_params=pltpu.CompilerParams(vmem_limit_bytes=24 << 20),
        cost_estimate=pl.CostEstimate(flops=flops, bytes_accessed=n_bytes, transcendentals=0),
        name=name,
    )(*args)


def shape(dims, dtype):
    return jax.ShapeDtypeStruct(dims, dtype)


def place():
    col = lax.axis_index("col")
    return lax.axis_index("row"), col // 2, col % 2


def panel_at(starts_ref, count, slot):
    found = jnp.int32(0)
    for p in range(count):
        found = jnp.where(starts_ref[p] == slot, jnp.int32(p), found)
    return found


def prep_kernel(count, width, starts_ref, grad_ref, out_ref):
    for slot in range(count):
        begin = pl.multiple_of(panel_at(starts_ref, count, slot) * width, width)
        out_ref[slot] = grad_ref[:, pl.ds(begin, width)].astype(out_ref.dtype)


def pack_kernel(count, width, mine_ref, other_ref, *out_refs):
    _, z, h = place()
    lanes = lax.broadcasted_iota(jnp.int32, mine_ref.shape[1:], 1)
    low = lanes < width // 2
    for k in range(count):
        slot = lax.rem(z + k, count)
        mine = mine_ref[slot].astype(F32)
        other = other_ref[slot].astype(F32)
        first = jnp.where(h == 0, mine, pltpu.roll(other, width // 2, 1))
        second = jnp.where(h == 0, pltpu.roll(other, width // 2, 1), mine)
        out_refs[k][...] = jnp.where(low, first, second).astype(out_refs[k].dtype)


def solve(x_ref, xb_ref, rhs, own_ref, other_ref):
    half = own_ref.shape[1]
    left = jnp.dot(rhs, own_ref[...], preferred_element_type=F32)
    right = jnp.dot(rhs, other_ref[...], preferred_element_type=F32)
    x_ref[:, :half] = left
    x_ref[:, half:] = right
    xb_ref[:, :half] = left.astype(BF16)
    xb_ref[:, half:] = right.astype(BF16)


def first_kernel(count, *refs):
    pieces = refs[:count]
    own_ref, other_ref, x_ref, xb_ref, acc_ref, natural = refs[count:]
    r, z, _ = place()
    rows, width = pieces[0].shape
    for k in range(count):
        source = lax.rem(z - k + count, count)
        piece = pieces[k][...].astype(F32)
        top = pl.multiple_of(source * (2 * rows), 8)
        natural[pl.ds(top, rows), :] = piece
        natural[pl.ds(pl.multiple_of(top + rows, 8), rows), :] = pltpu.roll(piece, width // 2, 1)
    acc_ref[...] = jnp.transpose(natural[...])[: width // 2]

    @pl.when(r == z)
    def _():
        solve(x_ref, xb_ref, acc_ref[...].astype(BF16), own_ref, other_ref)


def solve_kernel(tick, rhs_ref, own_ref, other_ref, x_ref, xb_ref):
    r, z, _ = place()

    @pl.when((r == z) & (z >= tick))
    def _():
        solve(x_ref, xb_ref, rhs_ref[...], own_ref, other_ref)


def product(x_ref, own_ref, other_ref):
    half = own_ref.shape[1]
    dims = (((1,), (1,)), ((), ()))
    left = lax.dot_general(x_ref[:, :half], own_ref[...], dims, preferred_element_type=F32)
    return left + lax.dot_general(x_ref[:, half:], other_ref[...], dims, preferred_element_type=F32)


def near_kernel(tick, x_ref, acc_ref, own_ref, other_ref, out_ref):
    r, z, _ = place()

    @pl.when((r == z + 1) & (z >= tick))
    def _():
        out_ref[...] = (acc_ref[...] - product(x_ref, own_ref, other_ref)).astype(out_ref.dtype)


def far_kernel(tick, acc_ref, own_ref, other_ref, *refs):
    x_refs, out_ref = refs[:-1], refs[-1]
    r, z, _ = place()
    for i, x_ref in enumerate(x_refs):

        @pl.when((r == z + 2 + i) & (z >= tick))
        def _():
            out_ref[...] = acc_ref[...] - product(x_ref, own_ref, other_ref)


def fold_kernel(count, x_ref, *refs):
    out_refs, natural = refs[:-1], refs[-1]
    _, z, h = place()
    rows, width = out_refs[0].shape
    half = x_ref.shape[1] // 2

    @pl.when(h == 0)
    def _():
        natural[: 2 * half, : width // 2] = jnp.transpose(x_ref[...])

    @pl.when(h == 1)
    def _():
        natural[half : 2 * half, : width // 2] = jnp.transpose(x_ref[:, :half])
        natural[:half, : width // 2] = jnp.transpose(x_ref[:, half:])

    lanes = lax.broadcasted_iota(jnp.int32, (rows, width), 1)
    for k in range(count):
        target = lax.rem(z + k, count)
        top = pl.multiple_of(target * (2 * rows), 8)
        upper = natural[pl.ds(top, rows), :]
        lower = natural[pl.ds(pl.multiple_of(top + rows, 8), rows), :]
        out_refs[k][...] = jnp.where(lanes < width // 2, upper, pltpu.roll(lower, width // 2, 1))


def pick_kernel(count, ticks, *refs):
    out_ref = refs[-1]
    early, last = refs[: (ticks - 1) * count], refs[(ticks - 1) * count : -1]
    r, z, _ = place()
    for t in range(ticks - 1):
        for k in range(count):

            @pl.when(lax.rem(z - r + count, count) == k)
            def _():
                out_ref[t] = early[t * count + k][...]

    for k in range(count):
        source = lax.rem(z - k + count, count)

        @pl.when((source >= ticks - 1) & (source <= r))
        def _():
            out_ref[source] = last[k][...]


def final_kernel(count, ticks, starts_ref, grad_ref, mine_ref, other_ref, out_ref):
    r, _, h = place()
    width = mine_ref.shape[2]
    lanes = lax.broadcasted_iota(jnp.int32, mine_ref.shape[1:], 1)
    for s in range(count):
        begin = pl.multiple_of(panel_at(starts_ref, count, s) * width, width)

        @pl.when(r < s)
        def _():
            out_ref[:, pl.ds(begin, width)] = grad_ref[:, pl.ds(begin, width)]

        @pl.when(r >= s)
        def _():
            slot = jnp.where(r - s <= ticks - 2, r - s, s + ticks - 1)
            mine = mine_ref[slot]
            other = pltpu.roll(other_ref[slot], width // 2, 1)
            low = jnp.where(h == 0, mine, other)
            high = jnp.where(h == 0, other, mine)
            out_ref[:, pl.ds(begin, width)] = jnp.where(lanes < width // 2, low, high)


def body(factor, gradient, starts):
    count = starts.shape[0]
    ticks = min(TICKS, count)
    rows = gradient.shape[0]
    width = gradient.shape[1] // count
    tile, half = factor.shape
    cols = width // 2
    devices = [(r, z, h) for r in range(count) for z in range(count) for h in range(2)]

    def move(array, target):
        pairs = []
        for r, z, h in devices:
            goal = target(r, z, h)
            if goal is not None:
                pairs.append(((r * count + z) * 2 + h, (goal[0] * count + goal[1]) * 2 + goal[2]))
        return lax.ppermute(array, ("row", "col"), pairs)

    def cores(array):
        return move(array, lambda r, z, h: (r, z, 1 - h))

    def along(array, k):
        return move(array, lambda r, z, h: (r, (z + k) % count, h))

    def across(array, d):
        return move(array, lambda r, z, h: ((r + d) % count, z, h))

    def to_next_row(array):
        def target(r, z, h):
            return (z % 2 + ((r - z % 2) % count ^ 1)) % count, z, h

        return move(array, target)

    def to_next_col(array):
        def target(r, z, h):
            if r % 2 == 1:
                return r, z ^ 1, h
            if z in (0, count - 1):
                return r ^ 2, z, h
            return r, ((z - 1) ^ 1) + 1, h

        return move(array, target)

    def far_to_next_col(array, tick):
        def target(r, z, h):
            return (r, z + 1, h) if r >= z + 2 and z >= tick else None

        return move(array, target)

    flops = 2 * cols * tile * tile
    other_tile = cores(factor)
    mine = call(
        lambda *a: prep_kernel(count, width, *a),
        [shape((count, rows, width), BF16)], (starts, gradient), [SM, VM], name="prep",
    )[0]
    theirs = cores(mine)
    pieces = call(
        lambda *a: pack_kernel(count, width, *a),
        [shape((rows, width), BF16)] * count, (mine, theirs), [VM, VM], name="pack",
    )
    arrived = [pieces[0]] + [along(pieces[k], k) for k in range(1, count)]
    wide = [shape((cols, tile), F32), shape((cols, tile), BF16)]
    x, xb, acc = call(
        lambda *a: first_kernel(count, *a),
        wide + [shape((cols, tile), F32)], (*arrived, factor, other_tile), [VM] * (count + 2),
        [pltpu.VMEM((tile, width), F32)], flops, "first",
    )
    early, last = [], None
    for tick in range(ticks):
        if tick:
            x, xb = call(
                lambda *a: solve_kernel(tick, *a),
                wide, (rhs, factor, other_tile), [VM] * 3, (), flops, "solve",
            )
        final = tick == ticks - 1
        result = x
        if count - 1 > tick:
            near = to_next_row(xb)
            far = [across(xb, d) for d in range(2, count - tick)]
            out = call(
                lambda *a: near_kernel(tick, *a),
                [shape((cols, tile), F32 if final else BF16)], (near, acc, factor, other_tile),
                [VM] * 4, (), flops, "near",
            )[0]
            if final:
                r, z, _ = place()
                result = jnp.where(r == z, x, out)
            else:
                rhs = to_next_col(out)
            if far:
                out = call(
                    lambda *a: far_kernel(tick, *a),
                    [shape((cols, tile), F32)], (acc, factor, other_tile, *far),
                    [VM] * (3 + len(far)), (), flops, "far",
                )[0]
                if final:
                    result = jnp.where(r >= z + 2, out, result)
                else:
                    acc = far_to_next_col(out, tick)
        parts = call(
            lambda *a: fold_kernel(count, *a),
            [shape((rows, width), F32)] * count, (result,), [VM],
            [pltpu.VMEM((tile, width), F32)], 0, "fold",
        )
        sent = [parts[0]] + [along(parts[k], k) for k in range(1, count)]
        if final:
            last = sent
        else:
            early += sent
    slots = max(count, ticks)
    mine = call(
        lambda *a: pick_kernel(count, ticks, *a),
        [shape((slots, rows, width), F32)], (*early, *last), [VM] * (count * ticks), name="pick",
    )[0]
    theirs = cores(mine)
    return call(
        lambda *a: final_kernel(count, ticks, *a),
        [shape(gradient.shape, F32)], (starts, gradient, mine, theirs), [SM, VM, VM, VM], name="final",
    )[0]


def solution(mesh):
    in_specs = (P("row", "col"), P(("row", "col"), None), P())
    out_specs = P(("row", "col"), None)
    return jax.shard_map(body, mesh=mesh, in_specs=in_specs, out_specs=out_specs, check_vma=False)
```

```python
import jax
import jax.numpy as jnp
from jax import lax
from jax.experimental import pallas as pl
from jax.experimental.pallas import tpu as pltpu
from jax.sharding import PartitionSpec as P


TICKS = 6
F32 = jnp.float32
BF16 = jnp.bfloat16
VM = pl.BlockSpec(memory_space=pltpu.VMEM)
SM = pl.BlockSpec(memory_space=pltpu.SMEM)


def call(kernel, outs, args, specs, scratch=(), flops=0):
    n_bytes = sum(o.size * o.dtype.itemsize for o in outs)
    return pl.pallas_call(
        kernel,
        out_shape=outs,
        in_specs=specs,
        out_specs=[VM] * len(outs),
        scratch_shapes=list(scratch),
        compiler_params=pltpu.CompilerParams(vmem_limit_bytes=24 << 20),
        cost_estimate=pl.CostEstimate(flops=flops, bytes_accessed=n_bytes, transcendentals=0),
    )(*args)


def shape(dims, dtype):
    return jax.ShapeDtypeStruct(dims, dtype)


def place():
    col = lax.axis_index("col")
    return lax.axis_index("row"), col // 2, col % 2


def panel_at(starts_ref, count, slot):
    found = jnp.int32(0)
    for p in range(count):
        found = jnp.where(starts_ref[p] == slot, jnp.int32(p), found)
    return found


def prep_kernel(count, width, starts_ref, grad_ref, out_ref):
    for slot in range(count):
        begin = pl.multiple_of(panel_at(starts_ref, count, slot) * width, width)
        out_ref[slot] = grad_ref[:, pl.ds(begin, width)].astype(out_ref.dtype)


def pack_kernel(count, width, mine_ref, other_ref, *out_refs):
    _, z, h = place()
    lanes = lax.broadcasted_iota(jnp.int32, mine_ref.shape[1:], 1)
    low = lanes < width // 2
    for k in range(count):
        slot = z ^ k
        mine = mine_ref[slot].astype(F32)
        other = other_ref[slot].astype(F32)
        first = jnp.where(h == 0, mine, pltpu.roll(other, width // 2, 1))
        second = jnp.where(h == 0, pltpu.roll(other, width // 2, 1), mine)
        out_refs[k][...] = jnp.where(low, first, second).astype(out_refs[k].dtype)


def solve(x_ref, xb_ref, rhs, own_ref, other_ref):
    half = own_ref.shape[1]
    left = jnp.dot(rhs, own_ref[...], preferred_element_type=F32)
    right = jnp.dot(rhs, other_ref[...], preferred_element_type=F32)
    x_ref[:, :half] = left
    x_ref[:, half:] = right
    xb_ref[:, :half] = left.astype(BF16)
    xb_ref[:, half:] = right.astype(BF16)


def solve(rhs, own_ref, other_ref, x_ref, xb_ref):
    half = own_ref.shape[1]
    left = jnp.dot(rhs, own_ref[...], preferred_element_type=F32)
    right = jnp.dot(rhs, other_ref[...], preferred_element_type=F32)
    xb_ref[:, :half] = left.astype(BF16)
    xb_ref[:, half:] = right.astype(BF16)
    x_ref[:, :half] = left
    x_ref[:, half:] = right


def load_kernel(tile_ref, _, out_ref, sem):
    copy = pltpu.make_async_copy(tile_ref, out_ref, sem)
    copy.start()
    copy.wait()


def first_kernel(count, *refs):
    pieces = refs[:count]
    own_ref, other_ref, x_ref, xb_ref, grad_ref, natural = refs[count:]
    r, z, _ = place()
    rows, width = pieces[0].shape
    for k in range(count):
        source = z ^ k
        piece = pieces[k][...].astype(F32)
        top = pl.multiple_of(source * (2 * rows), 8)
        natural[pl.ds(top, rows), :] = piece
        natural[pl.ds(pl.multiple_of(top + rows, 8), rows), :] = pltpu.roll(piece, width // 2, 1)
    grad_ref[...] = jnp.transpose(natural[...])[: width // 2].astype(BF16)

    @pl.when(r == z)
    def _():
        solve(grad_ref[...], own_ref, other_ref, x_ref, xb_ref)


def solve_kernel(tick, rhs_ref, own_ref, other_ref, x_ref, xb_ref):
    r, z, _ = place()

    @pl.when((r == z) & (z >= tick))
    def _():
        solve(rhs_ref[...], own_ref, other_ref, x_ref, xb_ref)


def turn_kernel(own_ref, other_ref, _, out_ref):
    r, z, _ = place()
    half = own_ref.shape[1]

    @pl.when(r > z)
    def _():
        out_ref[:half] = jnp.transpose(own_ref[...])
        out_ref[half:] = jnp.transpose(other_ref[...])


def near_kernel(tick, x_ref, grad_ref, turned_ref, *refs):
    out_ref = refs[-1]
    r, z, _ = place()

    @pl.when((r == z + 1) & (z >= tick))
    def _():
        value = grad_ref[...].astype(F32)
        if tick:
            value = value - refs[0][...].astype(F32)
        value = value - jnp.dot(x_ref[...], turned_ref[...], preferred_element_type=F32)
        out_ref[...] = value.astype(out_ref.dtype)


def far_kernel(tick, final, turned_ref, *refs):
    out_ref = refs[-1]
    before = refs[0] if tick else None
    grad_ref = refs[1] if final else None
    x_refs = refs[(1 if tick else 0) + (1 if final else 0) : -1]
    r, z, _ = place()
    for i, x_ref in enumerate(x_refs):

        @pl.when((r == z + 2 + i) & (z >= tick))
        def _():
            value = jnp.dot(x_ref[...], turned_ref[...], preferred_element_type=F32)
            if before is not None:
                value = value + before[...].astype(F32)
            if grad_ref is not None:
                value = grad_ref[...].astype(F32) - value
            out_ref[...] = value.astype(out_ref.dtype)


def fold(x_ref, natural):
    _, _, h = place()
    half, width = x_ref.shape[1] // 2, natural.shape[1]

    @pl.when(h == 0)
    def _():
        natural[: 2 * half, : width // 2] = jnp.transpose(x_ref[...])

    @pl.when(h == 1)
    def _():
        natural[half : 2 * half, : width // 2] = jnp.transpose(x_ref[:, :half])
        natural[:half, : width // 2] = jnp.transpose(x_ref[:, half:])


def folded(natural, rows, target):
    width = natural.shape[1]
    lanes = lax.broadcasted_iota(jnp.int32, (rows, width), 1)
    top = pl.multiple_of(target * (2 * rows), 8)
    upper = natural[pl.ds(top, rows), :]
    lower = natural[pl.ds(pl.multiple_of(top + rows, 8), rows), :]
    return jnp.where(lanes < width // 2, upper, pltpu.roll(lower, width // 2, 1))


def early_kernel(count, n_parts, *refs):
    x_refs, out_refs, natural = refs[:n_parts], refs[n_parts:-1], refs[-1]
    r, z, _ = place()
    rows = out_refs[0].shape[1]

    @pl.when(r == z)
    def _():
        for t in range(n_parts):
            fold(x_refs[t], natural)
            for k in range(count):
                out_refs[k][t] = folded(natural, rows, z ^ k)


def last_kernel(count, x_ref, *refs):
    out_refs, natural = refs[:-1], refs[-1]
    _, z, _ = place()
    rows = out_refs[0].shape[0]
    fold(x_ref, natural)
    for k in range(count):
        out_refs[k][...] = folded(natural, rows, z ^ k).astype(out_refs[k].dtype)


def pick_early_kernel(count, *refs):
    out_ref = refs[-1]
    r, z, _ = place()
    first = 0
    for group in range(0, len(refs) - 1, count):
        parts = refs[group].shape[0]
        for k in range(count):

            @pl.when((z ^ r) == k)
            def _():
                out_ref[first : first + parts] = refs[group + k][...]

        first += parts


def pick_last_kernel(count, ticks, *refs):
    out_ref = refs[-1]
    r, z, _ = place()
    for k in range(count):
        source = z ^ k

        @pl.when((source >= ticks - 1) & (source <= r))
        def _():
            out_ref[source - (ticks - 1)] = refs[k][...]


def join(mine, other, h):
    width = mine.shape[1]
    lanes = lax.broadcasted_iota(jnp.int32, mine.shape, 1)
    other = pltpu.roll(other.astype(F32), width // 2, 1)
    mine = mine.astype(F32)
    low = jnp.where(h == 0, mine, other)
    high = jnp.where(h == 0, other, mine)
    return jnp.where(lanes < width // 2, low, high)


def put_early_kernel(count, ticks, starts_ref, grad_ref, mine_ref, other_ref, out_ref):
    r, _, h = place()
    width = mine_ref.shape[2]
    for s in range(count):
        begin = pl.multiple_of(panel_at(starts_ref, count, s) * width, width)

        @pl.when(r < s)
        def _():
            out_ref[:, pl.ds(begin, width)] = grad_ref[:, pl.ds(begin, width)]

        @pl.when((r >= s) & (r - s <= ticks - 2))
        def _():
            t = r - s
            out_ref[:, pl.ds(begin, width)] = join(mine_ref[t], other_ref[t], h)


def put_last_kernel(count, ticks, starts_ref, early_ref, mine_ref, other_ref, out_ref):
    r, _, h = place()
    width = mine_ref.shape[2]
    out_ref[...] = early_ref[...]
    for s in range(count - ticks + 1):
        begin = pl.multiple_of(panel_at(starts_ref, count, s) * width, width)

        @pl.when(r - s >= ticks - 1)
        def _():
            out_ref[:, pl.ds(begin, width)] = join(mine_ref[s], other_ref[s], h)


def early_groups(ticks):
    if ticks < 3:
        return {ticks - 2: list(range(ticks - 1))}
    groups = {t: [t - 1] for t in range(1, ticks - 1)}
    groups[ticks - 2].append(ticks - 2)
    return groups


def body(factor, gradient, starts):
    count = starts.shape[0]
    ticks = min(TICKS, count)
    rows = gradient.shape[0]
    width = gradient.shape[1] // count
    tile, _ = factor.shape
    cols = width // 2
    devices = [(r, z, h) for r in range(count) for z in range(count) for h in range(2)]

    def move(array, target):
        pairs = []
        for r, z, h in devices:
            goal = target(r, z, h)
            if goal is not None:
                pairs.append(((r * count + z) * 2 + h, (goal[0] * count + goal[1]) * 2 + goal[2]))
        return lax.ppermute(array, ("row", "col"), pairs)

    def cores(array):
        return move(array, lambda r, z, h: (r, z, 1 - h))

    def along(array, k):
        return move(array, lambda r, z, h: (r, z ^ k, h))

    def from_diagonal(array, k):
        return move(array, lambda r, z, h: (r, z ^ k, h) if r == z else None)

    def to_far_row(array, tick, d):
        def target(r, z, h):
            return (r + d, z, h) if r == z and z >= tick and r + d < count else None

        return move(array, target)

    def to_next_row(array):
        def target(r, z, h):
            return (z % 2 + ((r - z % 2) % count ^ 1)) % count, z, h

        return move(array, target)

    def to_next_col(array):
        def target(r, z, h):
            base = z - z % 2 if r % 2 else z - 1 + z % 2
            if base < 0 or base + 1 >= count:
                return r ^ 2, z, h
            lead = (r ^ 2) == base + 1 or (r != base + 1 and r & 2)
            if (z == base) == (not lead):
                return r, base + 1 if z == base else base, h
            return r ^ 2, z, h

        return move(array, target)

    def far_to_next_col(array, tick):
        def target(r, z, h):
            return (r, z + 1, h) if r >= z + 2 and z >= tick else None

        return move(array, target)

    flops = 2 * cols * tile * tile
    mine = call(
        lambda *a: prep_kernel(count, width, *a),
        [shape((count, rows, width), BF16)], (starts, gradient), [SM, VM],
    )[0]
    theirs = cores(mine)
    pieces = call(
        lambda *a: pack_kernel(count, width, *a),
        [shape((rows, width), BF16)] * count, (mine, theirs), [VM, VM],
    )
    arrived = [pieces[0]] + [along(pieces[k], k) for k in range(1, count)]
    other_tile = cores(factor)
    own_tile = call(
        load_kernel, [shape(factor.shape, BF16)], (factor, pieces[0]),
        [pl.BlockSpec(memory_space=pl.ANY), VM], [pltpu.SemaphoreType.DMA],
    )[0]
    wide = [shape((cols, tile), F32), shape((cols, tile), BF16)]
    x, xb, grad = call(
        lambda *a: first_kernel(count, *a),
        wide + [shape((cols, tile), BF16)], (*arrived, own_tile, other_tile), [VM] * (count + 2),
        [pltpu.VMEM((tile, width), F32)], flops,
    )
    turned = call(turn_kernel, [shape((tile, tile), BF16)], (own_tile, other_tile, xb), [VM] * 3)[0]
    groups = early_groups(ticks) if ticks > 1 else {}
    xs, before, sent_early = [], None, []
    for tick in range(ticks):
        final = tick == ticks - 1
        if tick:
            x, xb = call(
                lambda *a: solve_kernel(tick, *a),
                wide, (rhs, own_tile, other_tile), [VM] * 3, (), flops,
            )
        result = x
        xs.append(x)
        if count - 1 > tick:
            dtype = F32 if final else BF16
            near = to_next_row(xb)
            far = [to_far_row(xb, tick, d) for d in range(2, count - tick)]
            carried = [before] if tick else []
            out = call(
                lambda *a: near_kernel(tick, *a),
                [shape((cols, tile), dtype)], (near, grad, turned, *carried),
                [VM] * (3 + len(carried)), (), flops,
            )[0]
            if final:
                r, z, _ = place()
                result = jnp.where(r == z, x, out)
                carried = carried + [grad]
            else:
                rhs = to_next_col(out)
            if far:
                if not final:
                    grad = far_to_next_col(grad, tick)
                out = call(
                    lambda *a: far_kernel(tick, final, *a),
                    [shape((cols, tile), dtype)], (turned, *carried, *far),
                    [VM] * (1 + len(carried) + len(far)), (), flops,
                )[0]
                if final:
                    result = jnp.where(r >= z + 2, out, result)
                else:
                    before = far_to_next_col(out, tick)
        if tick in groups:
            members = groups[tick]
            parts = call(
                lambda *a: early_kernel(count, len(members), *a),
                [shape((len(members), rows, width), F32)] * count, tuple(xs[t] for t in members),
                [VM] * len(members), [pltpu.VMEM((tile, width), F32)],
            )
            sent_early += [parts[0]]
            sent_early += [from_diagonal(parts[k], k) for k in range(1, count)]
    parts = call(
        lambda *a: last_kernel(count, *a),
        [shape((rows, width), BF16)] * count, (result,), [VM],
        [pltpu.VMEM((tile, width), F32)],
    )
    sent = [parts[0]] + [along(parts[k], k) for k in range(1, count)]
    mine = call(
        lambda *a: pick_early_kernel(count, *a),
        [shape((ticks - 1, rows, width), F32)], sent_early, [VM] * len(sent_early),
    )[0]
    theirs = cores(mine)
    early = call(
        lambda *a: put_early_kernel(count, ticks, *a),
        [shape(gradient.shape, F32)], (starts, gradient, mine, theirs), [SM, VM, VM, VM],
    )[0]
    mine = call(
        lambda *a: pick_last_kernel(count, ticks, *a),
        [shape((count - ticks + 1, rows, width), BF16)], sent, [VM] * count,
    )[0]
    theirs = cores(mine)
    return call(
        lambda *a: put_last_kernel(count, ticks, *a),
        [shape(gradient.shape, F32)], (starts, early, mine, theirs), [SM, VM, VM, VM],
    )[0]


def solution(mesh):
    in_specs = (P("row", "col"), P(("row", "col"), None), P())
    out_specs = P(("row", "col"), None)

    return jax.shard_map(body, mesh=mesh, in_specs=in_specs, out_specs=out_specs, check_vma=False)
```

```python
import jax
import jax.numpy as jnp
from jax import lax
from jax.experimental import pallas as pl
from jax.experimental.pallas import tpu as pltpu
from jax.sharding import PartitionSpec as P


TICKS = 6
CHUNKS = 2
F32 = jnp.float32
BF16 = jnp.bfloat16
VM = pl.BlockSpec(memory_space=pltpu.VMEM)
SM = pl.BlockSpec(memory_space=pltpu.SMEM)


def call(kernel, outs, args, specs, scratch=(), flops=0, out_spec=VM, aliases=()):
    n_bytes = sum(o.size * o.dtype.itemsize for o in outs)
    return pl.pallas_call(
        kernel,
        out_shape=outs,
        in_specs=specs,
        out_specs=[out_spec] * len(outs),
        input_output_aliases=dict(aliases),
        scratch_shapes=list(scratch),
        compiler_params=pltpu.CompilerParams(vmem_limit_bytes=24 << 20),
        cost_estimate=pl.CostEstimate(flops=flops, bytes_accessed=n_bytes, transcendentals=0),
    )(*args)


def shape(dims, dtype):
    return jax.ShapeDtypeStruct(dims, dtype)


def place():
    col = lax.axis_index("col")
    return lax.axis_index("row"), col // 2, col % 2


def panel_at(starts_ref, count, slot):
    found = jnp.int32(0)
    for p in range(count):
        found = jnp.where(starts_ref[p] == slot, jnp.int32(p), found)
    return found


def prep_kernel(count, width, starts_ref, grad_ref, out_ref):
    for slot in range(count):
        begin = pl.multiple_of(panel_at(starts_ref, count, slot) * width, width)
        out_ref[slot] = grad_ref[:, pl.ds(begin, width)].astype(out_ref.dtype)


def pack_kernel(count, width, mine_ref, other_ref, *out_refs):
    _, z, h = place()
    lanes = lax.broadcasted_iota(jnp.int32, mine_ref.shape[1:], 1)
    low = lanes < width // 2
    for k in range(count):
        slot = z ^ k
        mine = mine_ref[slot].astype(F32)
        other = other_ref[slot].astype(F32)
        first = jnp.where(h == 0, mine, pltpu.roll(other, width // 2, 1))
        second = jnp.where(h == 0, pltpu.roll(other, width // 2, 1), mine)
        out_refs[k][...] = jnp.where(low, first, second).astype(out_refs[k].dtype)


def solve(x_ref, xb_ref, rhs, own_ref, other_ref):
    half = own_ref.shape[1]
    left = jnp.dot(rhs, own_ref[...], preferred_element_type=F32)
    right = jnp.dot(rhs, other_ref[...], preferred_element_type=F32)
    x_ref[:, :half] = left
    x_ref[:, half:] = right
    xb_ref[:, :half] = left.astype(BF16)
    xb_ref[:, half:] = right.astype(BF16)


def solve(rhs, own_ref, other_ref, x_ref, xb_ref):
    half = own_ref.shape[1]
    for side, tile_ref in ((slice(0, half), own_ref), (slice(half, 2 * half), other_ref)):
        value = jnp.dot(rhs, tile_ref[...], preferred_element_type=F32)
        x_ref[:, side] = value
        if xb_ref is not None:
            xb_ref[:, side] = value.astype(BF16)


def load_kernel(tile_ref, _, out_ref, sem):
    copy = pltpu.make_async_copy(tile_ref, out_ref, sem)
    copy.start()
    copy.wait()


def first_kernel(count, *refs):
    pieces = refs[:count]
    own_ref, other_ref, x_ref, xb_ref, grad_ref, natural = refs[count:]
    r, z, _ = place()
    rows, width = pieces[0].shape
    for k in range(count):
        source = z ^ k
        piece = pieces[k][...].astype(F32)
        top = pl.multiple_of(source * (2 * rows), 8)
        natural[pl.ds(top, rows), :] = piece
        natural[pl.ds(pl.multiple_of(top + rows, 8), rows), :] = pltpu.roll(piece, width // 2, 1)
    grad_ref[...] = jnp.transpose(natural[...])[: width // 2].astype(BF16)

    @pl.when(r == z)
    def _():
        solve(grad_ref[: x_ref.shape[0]], own_ref, other_ref, x_ref, xb_ref)


def solve_kernel(tick, top, n_before, rhs_ref, own_ref, other_ref, *refs):
    r, z, _ = place()
    before, outs = refs[:n_before], refs[n_before:]
    x_ref, xb_ref = outs[0], outs[1] if len(outs) > 1 else None
    rows = x_ref.shape[0]

    @pl.when((r == z) & (z >= tick))
    def _():
        solve(rhs_ref[top : top + rows], own_ref, other_ref, x_ref, xb_ref)
        if len(outs) > 2:
            for c, ref in enumerate(before):
                outs[2][c * rows : (c + 1) * rows] = ref[...]
            outs[2][n_before * rows :] = xb_ref[...]


def turn_kernel(own_ref, other_ref, _, out_ref):
    r, z, _ = place()
    half = own_ref.shape[1]

    @pl.when(r > z)
    def _():
        out_ref[:half] = jnp.transpose(own_ref[...])
        out_ref[half:] = jnp.transpose(other_ref[...])


def near_kernel(tick, c, x_ref, grad_ref, turned_ref, *refs):
    out_ref = refs[-1]
    rows = out_ref.shape[0]
    mine = slice(c * rows, (c + 1) * rows)
    r, z, _ = place()

    @pl.when((r == z + 1) & (z >= tick))
    def _():
        value = grad_ref[mine].astype(F32)
        if tick:
            value = value - refs[0][mine].astype(F32)
        value = value - jnp.dot(x_ref[...], turned_ref[...], preferred_element_type=F32)
        out_ref[...] = value.astype(out_ref.dtype)


def far_kernel(tick, final, turned_ref, *refs):
    out_ref = refs[-1]
    before = refs[0] if tick else None
    grad_ref = refs[1] if final else None
    x_refs = refs[(1 if tick else 0) + (1 if final else 0) : -1]
    r, z, _ = place()
    for i, x_ref in enumerate(x_refs):

        @pl.when((r == z + 2 + i) & (z >= tick))
        def _():
            value = jnp.dot(x_ref[...], turned_ref[...], preferred_element_type=F32)
            if before is not None:
                value = value + before[...].astype(F32)
            if grad_ref is not None:
                value = grad_ref[...].astype(F32) - value
            out_ref[...] = value.astype(out_ref.dtype)


def fold(x_refs, natural):
    _, _, h = place()
    half, width = x_refs[0].shape[1] // 2, natural.shape[1]
    own = jnp.concatenate([ref[:, :half] for ref in x_refs], axis=0)
    other = jnp.concatenate([ref[:, half:] for ref in x_refs], axis=0)
    top = pl.multiple_of(h * half, 8)
    natural[pl.ds(top, half), : width // 2] = jnp.transpose(own)
    natural[pl.ds(pl.multiple_of(half - top, 8), half), : width // 2] = jnp.transpose(other)


def folded(natural, rows, target):
    width = natural.shape[1]
    lanes = lax.broadcasted_iota(jnp.int32, (rows, width), 1)
    top = pl.multiple_of(target * (2 * rows), 8)
    upper = natural[pl.ds(top, rows), :]
    lower = natural[pl.ds(pl.multiple_of(top + rows, 8), rows), :]
    return jnp.where(lanes < width // 2, upper, pltpu.roll(lower, width // 2, 1))


def early_kernel(count, n_chunks, *refs):
    x_refs, out_refs, natural = refs[: -count - 1], refs[-count - 1 : -1], refs[-1]
    r, z, _ = place()
    rows = out_refs[0].shape[1]

    @pl.when(r == z)
    def _():
        for t in range(len(x_refs) // n_chunks):
            fold(x_refs[t * n_chunks : (t + 1) * n_chunks], natural)
            for k in range(count):
                out_refs[k][t] = folded(natural, rows, z ^ k).astype(out_refs[k].dtype)


def last_kernel(count, ticks, n_before, solves, *refs):
    before, refs = refs[:n_before], refs[n_before:]
    r, z, _ = place()
    if solves:
        rhs_ref, own_ref, other_ref = refs[:3]
        out_refs, natural, x_ref = refs[3:-2], refs[-2], refs[-1]
    else:
        out_refs, natural = refs[:-1], refs[-1]
    rows = out_refs[0].shape[0]

    @pl.when((z >= ticks - 1) & (z <= r))
    def _():
        x_refs = list(before)
        if solves:
            solve(rhs_ref[...], own_ref, other_ref, x_ref, None)
            x_refs.append(x_ref)
        fold(x_refs, natural)
        for k in range(count):
            out_refs[k][...] = folded(natural, rows, z ^ k).astype(out_refs[k].dtype)


def pick_early_kernel(count, *refs):
    out_ref = refs[-1]
    r, z, _ = place()
    for k in range(count):

        @pl.when((z ^ r) == k)
        def _():
            out_ref[...] = refs[k][...]


def pick_last_kernel(count, ticks, *refs):
    out_ref = refs[-1]
    r, z, _ = place()
    for k in range(count):
        source = z ^ k

        @pl.when((source >= ticks - 1) & (source <= r))
        def _():
            out_ref[source - (ticks - 1)] = refs[k][...]


def join(mine, other, h):
    width = mine.shape[1]
    lanes = lax.broadcasted_iota(jnp.int32, mine.shape, 1)
    other = pltpu.roll(other.astype(F32), width // 2, 1)
    mine = mine.astype(F32)
    low = jnp.where(h == 0, mine, other)
    high = jnp.where(h == 0, other, mine)
    return jnp.where(lanes < width // 2, low, high)


def put_early_kernel(count, ticks, starts_ref, grad_ref, mine_ref, other_ref, out_ref):
    r, _, h = place()
    width = mine_ref.shape[2]
    for s in range(count):
        begin = pl.multiple_of(panel_at(starts_ref, count, s) * width, width)

        @pl.when(r < s)
        def _():
            out_ref[:, pl.ds(begin, width)] = grad_ref[:, pl.ds(begin, width)]

        @pl.when((r >= s) & (r - s <= ticks - 2))
        def _():
            t = r - s
            out_ref[:, pl.ds(begin, width)] = join(mine_ref[t], other_ref[t], h)


def put_last_kernel(count, ticks, starts_ref, _, mine_ref, other_ref, out_ref, joined, sem):
    r, _, h = place()
    width = mine_ref.shape[2]
    for s in range(count - ticks + 1):
        begin = pl.multiple_of(panel_at(starts_ref, count, s) * width, width)

        @pl.when(r - s >= ticks - 1)
        def _():
            joined[...] = join(mine_ref[s], other_ref[s], h)
            copy = pltpu.make_async_copy(joined, out_ref.at[:, pl.ds(begin, width)], sem)
            copy.start()
            copy.wait()


def body(factor, gradient, starts):
    count = starts.shape[0]
    ticks = min(TICKS, count)
    rows = gradient.shape[0]
    width = gradient.shape[1] // count
    tile, _ = factor.shape
    cols = width // 2
    devices = [(r, z, h) for r in range(count) for z in range(count) for h in range(2)]

    def move(array, target):
        pairs = []
        for r, z, h in devices:
            goal = target(r, z, h)
            if goal is not None:
                pairs.append(((r * count + z) * 2 + h, (goal[0] * count + goal[1]) * 2 + goal[2]))
        return lax.ppermute(array, ("row", "col"), pairs)

    def cores(array):
        return move(array, lambda r, z, h: (r, z, 1 - h))

    def along(array, k):
        return move(array, lambda r, z, h: (r, z ^ k, h))

    def from_diagonal(array, k):
        return move(array, lambda r, z, h: (r, z ^ k, h) if r == z else None)

    def to_far_row(array, tick, d):
        def target(r, z, h):
            return (r + d, z, h) if r == z and z >= tick and r + d < count else None

        return move(array, target)

    def to_next_row(array, tick):
        def target(r, z, h):
            return (r + 1, z, h) if r == z and z >= tick and r + 1 < count else None

        return move(array, target)

    def to_next_col(array):
        def target(r, z, h):
            base = z - z % 2 if r % 2 else z - 1 + z % 2
            if base < 0 or base + 1 >= count:
                return r ^ 2, z, h
            lead = (r ^ 2) == base + 1 or (r != base + 1 and r & 2)
            if (z == base) == (not lead):
                return r, base + 1 if z == base else base, h
            return r ^ 2, z, h

        return move(array, target)

    def from_last(array, k):
        def target(r, z, h):
            return (r, z ^ k, h) if ticks - 1 <= z <= r else None

        return move(array, target)

    def far_to_next_col(array, tick):
        def target(r, z, h):
            return (r, z + 1, h) if r >= z + 2 and z >= tick else None

        return move(array, target)

    flops = 2 * cols * tile * tile
    mine = call(
        lambda *a: prep_kernel(count, width, *a),
        [shape((count, rows, width), BF16)], (starts, gradient), [SM, VM],
    )[0]
    theirs = cores(mine)
    pieces = call(
        lambda *a: pack_kernel(count, width, *a),
        [shape((rows, width), BF16)] * count, (mine, theirs), [VM, VM],
    )
    arrived = [pieces[0]] + [along(pieces[k], k) for k in range(1, count)]
    other_tile = cores(factor)
    own_tile = call(
        load_kernel, [shape(factor.shape, BF16)], (factor, pieces[0]),
        [pl.BlockSpec(memory_space=pl.ANY), VM], [pltpu.SemaphoreType.DMA],
    )[0]
    part = cols // CHUNKS
    pair = [shape((part, tile), F32), shape((part, tile), BF16)]
    scratch = [pltpu.VMEM((tile, width), F32)]
    x, xb, grad = call(
        lambda *a: first_kernel(count, *a),
        pair + [shape((cols, tile), BF16)], (*arrived, own_tile, other_tile), [VM] * (count + 2),
        scratch, flops,
    )
    turned = call(
        turn_kernel, [shape((tile, tile), BF16)], (own_tile, other_tile, grad), [VM] * 3,
    )[0]
    xs, before, sent_early = [], None, []
    for tick in range(ticks):
        final = tick == ticks - 1
        rest = count - 1 > tick
        solved, solved_b, downs = [], [], []
        for c in range(CHUNKS):
            if tick or c:
                if final and not rest and c == CHUNKS - 1:
                    break
                source, top = (rhs[c], 0) if tick else (grad, c * part)
                joins = c == CHUNKS - 1 and CHUNKS > 1
                outs = pair + ([shape((cols, tile), BF16)] if joins else [])
                outs = outs if rest else outs[:1]
                given = solved_b if joins else []
                done = call(
                    lambda *a: solve_kernel(tick, top, len(given), *a),
                    outs, (source, own_tile, other_tile, *given), [VM] * (3 + len(given)), (), flops,
                )
                x, xb, whole = done[0], done[1 % len(done)], done[-1]
            else:
                whole = xb
            solved.append(x)
            solved_b.append(xb)
            if rest:
                downs.append(to_next_row(xb, tick))
        xs.append(solved)
        results = solved
        if rest:
            dtype = F32 if final else BF16
            far = [to_far_row(whole, tick, d) for d in range(2, count - tick)]
            carried = [before] if tick else []
            outs, rhs = [], []
            for c in range(CHUNKS):
                out = call(
                    lambda *a: near_kernel(tick, c, *a),
                    [shape((part, tile), dtype)], (downs[c], grad, turned, *carried),
                    [VM] * (3 + len(carried)), (), flops,
                )[0]
                outs.append(out)
                if not final:
                    rhs.append(to_next_col(out))
            if final:
                r, z, _ = place()
                results = [jnp.where(r == z, a, b) for a, b in zip(solved, outs)]
                carried = carried + [grad]
            if far:
                if not final:
                    grad = far_to_next_col(grad, tick)
                out = call(
                    lambda *a: far_kernel(tick, final, *a),
                    [shape((cols, tile), dtype)], (turned, *carried, *far),
                    [VM] * (1 + len(carried) + len(far)), (), flops,
                )[0]
                if final:
                    results = [
                        jnp.where(r >= z + 2, out[c * part : (c + 1) * part], results[c])
                        for c in range(CHUNKS)
                    ]
                else:
                    before = far_to_next_col(out, tick)
        if tick == ticks - 2:
            given = [x for solved in xs for x in solved]
            parts = call(
                lambda *a: early_kernel(count, CHUNKS, *a),
                [shape((ticks - 1, rows, width), BF16)] * count, given,
                [VM] * len(given), scratch,
            )
            sent_early = [parts[0]]
            sent_early += [from_diagonal(parts[k], k) for k in range(1, count)]
    given, more = list(results), []
    if not rest:
        given += [rhs[-1], own_tile, other_tile]
        more = [pltpu.VMEM((part, tile), F32)]
    parts = call(
        lambda *a: last_kernel(count, ticks, len(results), not rest, *a),
        [shape((rows, width), BF16)] * count, given, [VM] * len(given), scratch + more, flops,
    )
    sent = [parts[0]] + [from_last(parts[k], k) for k in range(1, count)]
    mine = call(
        lambda *a: pick_early_kernel(count, *a),
        [shape((ticks - 1, rows, width), BF16)], sent_early, [VM] * len(sent_early),
    )[0]
    theirs = cores(mine)
    early = call(
        lambda *a: put_early_kernel(count, ticks, *a),
        [shape(gradient.shape, F32)], (starts, gradient, mine, theirs), [SM, VM, VM, VM],
    )[0]
    mine = call(
        lambda *a: pick_last_kernel(count, ticks, *a),
        [shape((count - ticks + 1, rows, width), BF16)], sent, [VM] * count,
    )[0]
    theirs = cores(mine)
    hbm = pl.BlockSpec(memory_space=pltpu.HBM)
    return call(
        lambda *a: put_last_kernel(count, ticks, *a),
        [shape(gradient.shape, F32)], (starts, early, mine, theirs), [SM, hbm, VM, VM],
        [pltpu.VMEM((rows, width), F32), pltpu.SemaphoreType.DMA], 0, hbm, {1: 0},
    )[0]


def solution(mesh):
    in_specs = (P("row", "col"), P(("row", "col"), None), P())
    out_specs = P(("row", "col"), None)

    return jax.shard_map(body, mesh=mesh, in_specs=in_specs, out_specs=out_specs, check_vma=False)
```

```python
import jax
import jax.numpy as jnp
from jax import lax
from jax.experimental import pallas as pl
from jax.experimental.pallas import tpu as pltpu
from jax.sharding import PartitionSpec as P


TICKS = 6
CHUNKS = 2
F32 = jnp.float32
BF16 = jnp.bfloat16
VM = pl.BlockSpec(memory_space=pltpu.VMEM)
SM = pl.BlockSpec(memory_space=pltpu.SMEM)


def call(kernel, outs, args, specs, scratch=(), flops=0, out_spec=VM, aliases=()):
    n_bytes = sum(o.size * o.dtype.itemsize for o in outs)
    return pl.pallas_call(
        kernel,
        out_shape=outs,
        in_specs=specs,
        out_specs=[out_spec] * len(outs),
        input_output_aliases=dict(aliases),
        scratch_shapes=list(scratch),
        compiler_params=pltpu.CompilerParams(vmem_limit_bytes=24 << 20),
        cost_estimate=pl.CostEstimate(flops=flops, bytes_accessed=n_bytes, transcendentals=0),
    )(*args)


def shape(dims, dtype):
    return jax.ShapeDtypeStruct(dims, dtype)


def place():
    col = lax.axis_index("col")
    return lax.axis_index("row"), col // 2, col % 2


def panel_at(starts_ref, count, slot):
    found = jnp.int32(0)
    for p in range(count):
        found = jnp.where(starts_ref[p] == slot, jnp.int32(p), found)
    return found


def prep_kernel(count, width, starts_ref, grad_ref, out_ref):
    for slot in range(count):
        begin = pl.multiple_of(panel_at(starts_ref, count, slot) * width, width)
        out_ref[slot] = grad_ref[:, pl.ds(begin, width)].astype(out_ref.dtype)


def pack_kernel(count, width, mine_ref, other_ref, *out_refs):
    _, z, h = place()
    lanes = lax.broadcasted_iota(jnp.int32, mine_ref.shape[1:], 1)
    low = lanes < width // 2
    for k in range(count):
        slot = z ^ k
        mine = mine_ref[slot].astype(F32)
        other = other_ref[slot].astype(F32)
        first = jnp.where(h == 0, mine, pltpu.roll(other, width // 2, 1))
        second = jnp.where(h == 0, pltpu.roll(other, width // 2, 1), mine)
        out_refs[k][...] = jnp.where(low, first, second).astype(out_refs[k].dtype)


def solve(x_ref, xb_ref, rhs, own_ref, other_ref):
    half = own_ref.shape[1]
    left = jnp.dot(rhs, own_ref[...], preferred_element_type=F32)
    right = jnp.dot(rhs, other_ref[...], preferred_element_type=F32)
    x_ref[:, :half] = left
    x_ref[:, half:] = right
    xb_ref[:, :half] = left.astype(BF16)
    xb_ref[:, half:] = right.astype(BF16)


def solve(rhs, own_ref, other_ref, x_ref, xb_ref):
    half = own_ref.shape[1]
    for side, tile_ref in ((slice(0, half), own_ref), (slice(half, 2 * half), other_ref)):
        value = jnp.dot(rhs, tile_ref[...], preferred_element_type=F32)
        x_ref[:, side] = value
        if xb_ref is not None:
            xb_ref[:, side] = value.astype(BF16)


def load_kernel(tile_ref, _, out_ref, sem):
    copy = pltpu.make_async_copy(tile_ref, out_ref, sem)
    copy.start()
    copy.wait()


def first_kernel(count, *refs):
    pieces = refs[:count]
    own_ref, other_ref, x_ref, xb_ref, grad_ref, natural = refs[count:]
    r, z, _ = place()
    rows, width = pieces[0].shape
    for k in range(count):
        source = z ^ k
        piece = pieces[k][...].astype(F32)
        top = pl.multiple_of(source * (2 * rows), 8)
        natural[pl.ds(top, rows), :] = piece
        natural[pl.ds(pl.multiple_of(top + rows, 8), rows), :] = pltpu.roll(piece, width // 2, 1)
    grad_ref[...] = jnp.transpose(natural[...])[: width // 2].astype(BF16)

    @pl.when(r == z)
    def _():
        solve(grad_ref[: x_ref.shape[0]], own_ref, other_ref, x_ref, xb_ref)


def solve_kernel(tick, top, n_before, rhs_ref, own_ref, other_ref, *refs):
    r, z, _ = place()
    before, outs = refs[:n_before], refs[n_before:]
    x_ref, xb_ref = outs[0], outs[1] if len(outs) > 1 else None
    rows = x_ref.shape[0]

    @pl.when((r == z) & (z >= tick))
    def _():
        solve(rhs_ref[top : top + rows], own_ref, other_ref, x_ref, xb_ref)
        if len(outs) > 2:
            for c, ref in enumerate(before):
                outs[2][c * rows : (c + 1) * rows] = ref[...]
            outs[2][n_before * rows :] = xb_ref[...]


def turn_kernel(own_ref, other_ref, _, out_ref):
    r, z, _ = place()
    half = own_ref.shape[1]

    @pl.when(r > z)
    def _():
        out_ref[:half] = jnp.transpose(own_ref[...])
        out_ref[half:] = jnp.transpose(other_ref[...])


def near_kernel(tick, c, x_ref, grad_ref, turned_ref, *refs):
    out_ref = refs[-1]
    rows = out_ref.shape[0]
    mine = slice(c * rows, (c + 1) * rows)
    r, z, _ = place()

    @pl.when((r == z + 1) & (z >= tick))
    def _():
        value = grad_ref[mine].astype(F32)
        if tick:
            value = value - refs[0][mine].astype(F32)
        value = value - jnp.dot(x_ref[...], turned_ref[...], preferred_element_type=F32)
        out_ref[...] = value.astype(out_ref.dtype)


def far_kernel(tick, final, turned_ref, *refs):
    out_ref = refs[-1]
    before = refs[0] if tick else None
    grad_ref = refs[1] if final else None
    x_refs = refs[(1 if tick else 0) + (1 if final else 0) : -1]
    r, z, _ = place()
    for i, x_ref in enumerate(x_refs):

        @pl.when((r == z + 2 + i) & (z >= tick))
        def _():
            value = jnp.dot(x_ref[...], turned_ref[...], preferred_element_type=F32)
            if before is not None:
                value = value + before[...].astype(F32)
            if grad_ref is not None:
                value = grad_ref[...].astype(F32) - value
            out_ref[...] = value.astype(out_ref.dtype)


def fold(x_refs, natural):
    _, _, h = place()
    half, width = x_refs[0].shape[1] // 2, natural.shape[1]
    own = jnp.concatenate([ref[:, :half] for ref in x_refs], axis=0)
    other = jnp.concatenate([ref[:, half:] for ref in x_refs], axis=0)
    top = pl.multiple_of(h * half, 8)
    natural[pl.ds(top, half), : width // 2] = jnp.transpose(own)
    natural[pl.ds(pl.multiple_of(half - top, 8), half), : width // 2] = jnp.transpose(other)


def folded(natural, rows, target):
    width = natural.shape[1]
    lanes = lax.broadcasted_iota(jnp.int32, (rows, width), 1)
    top = pl.multiple_of(target * (2 * rows), 8)
    upper = natural[pl.ds(top, rows), :]
    lower = natural[pl.ds(pl.multiple_of(top + rows, 8), rows), :]
    return jnp.where(lanes < width // 2, upper, pltpu.roll(lower, width // 2, 1))


def early_kernel(count, n_chunks, *refs):
    x_refs, out_refs, natural = refs[: -count - 1], refs[-count - 1 : -1], refs[-1]
    r, z, _ = place()
    rows = out_refs[0].shape[1]

    @pl.when(r == z)
    def _():
        for t in range(len(x_refs) // n_chunks):
            fold(x_refs[t * n_chunks : (t + 1) * n_chunks], natural)
            for k in range(count):
                out_refs[k][t] = folded(natural, rows, z ^ k).astype(out_refs[k].dtype)


def last_kernel(count, ticks, n_before, solves, *refs):
    before, refs = refs[:n_before], refs[n_before:]
    r, z, _ = place()
    if solves:
        rhs_ref, own_ref, other_ref = refs[:3]
        out_refs, natural, x_ref = refs[3:-2], refs[-2], refs[-1]
    else:
        out_refs, natural = refs[:-1], refs[-1]
    rows = out_refs[0].shape[0]

    @pl.when((z >= ticks - 1) & (z <= r))
    def _():
        x_refs = list(before)
        if solves:
            solve(rhs_ref[...], own_ref, other_ref, x_ref, None)
            x_refs.append(x_ref)
        fold(x_refs, natural)
        for k in range(count):
            out_refs[k][...] = folded(natural, rows, z ^ k).astype(out_refs[k].dtype)


def pick_early_kernel(count, *refs):
    out_ref = refs[-1]
    r, z, _ = place()
    for k in range(count):

        @pl.when((z ^ r) == k)
        def _():
            out_ref[...] = refs[k][...]


def pick_last_kernel(count, ticks, *refs):
    out_ref = refs[-1]
    r, z, _ = place()
    for k in range(count):
        source = z ^ k

        @pl.when((source >= ticks - 1) & (source <= r))
        def _():
            out_ref[source - (ticks - 1)] = refs[k][...]


def join(mine, other, h):
    width = mine.shape[1]
    lanes = lax.broadcasted_iota(jnp.int32, mine.shape, 1)
    other = pltpu.roll(other.astype(F32), width // 2, 1)
    mine = mine.astype(F32)
    low = jnp.where(h == 0, mine, other)
    high = jnp.where(h == 0, other, mine)
    return jnp.where(lanes < width // 2, low, high)


def put_early_kernel(count, ticks, starts_ref, grad_ref, mine_ref, other_ref, out_ref, where_ref):
    r, _, h = place()
    width = mine_ref.shape[2]
    for s in range(count):
        panel = panel_at(starts_ref, count, s)
        where_ref[s] = jnp.full(where_ref.shape[1:], panel.astype(F32))
        begin = pl.multiple_of(panel * width, width)

        @pl.when(r < s)
        def _():
            out_ref[:, pl.ds(begin, width)] = grad_ref[:, pl.ds(begin, width)]

        @pl.when((r >= s) & (r - s <= ticks - 2))
        def _():
            t = r - s
            out_ref[:, pl.ds(begin, width)] = join(mine_ref[t], other_ref[t], h)


def put_last_kernel(count, ticks, where_ref, _, mine_ref, other_ref, out_ref, joined, sem):
    r, _, h = place()
    width = mine_ref.shape[2]
    for s in range(count - ticks + 1):

        @pl.when(r - s >= ticks - 1)
        def _():
            panel = jnp.max(where_ref[s]).astype(jnp.int32)
            begin = pl.multiple_of(panel * width, width)
            joined[...] = join(mine_ref[s], other_ref[s], h)
            copy = pltpu.make_async_copy(joined, out_ref.at[:, pl.ds(begin, width)], sem)
            copy.start()
            copy.wait()


def body(factor, gradient, starts):
    count = starts.shape[0]
    ticks = min(TICKS, count)
    rows = gradient.shape[0]
    width = gradient.shape[1] // count
    tile, _ = factor.shape
    cols = width // 2
    devices = [(r, z, h) for r in range(count) for z in range(count) for h in range(2)]

    def move(array, target):
        pairs = []
        for r, z, h in devices:
            goal = target(r, z, h)
            if goal is not None:
                pairs.append(((r * count + z) * 2 + h, (goal[0] * count + goal[1]) * 2 + goal[2]))
        return lax.ppermute(array, ("row", "col"), pairs)

    def cores(array):
        return move(array, lambda r, z, h: (r, z, 1 - h))

    def along(array, k):
        return move(array, lambda r, z, h: (r, z ^ k, h))

    def from_diagonal(array, k):
        return move(array, lambda r, z, h: (r, z ^ k, h) if r == z else None)

    def to_far_row(array, tick, d):
        def target(r, z, h):
            return (r + d, z, h) if r == z and z >= tick and r + d < count else None

        return move(array, target)

    def to_next_row(array):
        def target(r, z, h):
            idle, far = range(z - 1, -1, -1), range(count - 1, z + 1, -1)
            cycle = [z] + [z + 1] * (z + 1 < count) + [*far] + [*idle]
            return cycle[(cycle.index(r) + 1) % count], z, h

        return move(array, target)

    def to_next_col(array):
        def target(r, z, h):
            base = z - z % 2 if r % 2 else z - 1 + z % 2
            if base < 0 or base + 1 >= count:
                return r ^ 2, z, h
            lead = (r ^ 2) == base + 1 or (r != base + 1 and r & 2)
            if (z == base) == (not lead):
                return r, base + 1 if z == base else base, h
            return r ^ 2, z, h

        return move(array, target)

    def from_last(array, k):
        def target(r, z, h):
            return (r, z ^ k, h) if ticks - 1 <= z <= r else None

        return move(array, target)

    def far_to_next_col(array, tick):
        def target(r, z, h):
            return (r, z + 1, h) if r >= z + 2 and z >= tick else None

        return move(array, target)

    flops = 2 * cols * tile * tile
    mine = call(
        lambda *a: prep_kernel(count, width, *a),
        [shape((count, rows, width), BF16)], (starts, gradient), [SM, VM],
    )[0]
    theirs = cores(mine)
    pieces = call(
        lambda *a: pack_kernel(count, width, *a),
        [shape((rows, width), BF16)] * count, (mine, theirs), [VM, VM],
    )
    arrived = [pieces[0]] + [along(pieces[k], k) for k in range(1, count)]
    other_tile = cores(factor)
    own_tile = call(
        load_kernel, [shape(factor.shape, BF16)], (factor, pieces[0]),
        [pl.BlockSpec(memory_space=pl.ANY), VM], [pltpu.SemaphoreType.DMA],
    )[0]
    part = cols // CHUNKS
    pair = [shape((part, tile), F32), shape((part, tile), BF16)]
    scratch = [pltpu.VMEM((tile, width), F32)]
    x, xb, grad = call(
        lambda *a: first_kernel(count, *a),
        pair + [shape((cols, tile), BF16)], (*arrived, own_tile, other_tile), [VM] * (count + 2),
        scratch, flops,
    )
    turned = call(
        turn_kernel, [shape((tile, tile), BF16)], (own_tile, other_tile, pieces[0]), [VM] * 3,
    )[0]
    xs, before, sent_early = [], None, []
    for tick in range(ticks):
        final = tick == ticks - 1
        rest = count - 1 > tick
        solved, solved_b, downs = [], [], []
        for c in range(CHUNKS):
            if tick or c:
                if final and not rest and c == CHUNKS - 1:
                    break
                source, top = (rhs[c], 0) if tick else (grad, c * part)
                joins = c == CHUNKS - 1 and CHUNKS > 1 and count - 2 > tick
                outs = pair + ([shape((cols, tile), BF16)] if joins else [])
                outs = outs if rest else outs[:1]
                given = solved_b if joins else []
                done = call(
                    lambda *a: solve_kernel(tick, top, len(given), *a),
                    outs, (source, own_tile, other_tile, *given), [VM] * (3 + len(given)), (), flops,
                )
                x, xb, whole = done[0], done[1 % len(done)], done[-1]
            else:
                whole = xb
            solved.append(x)
            solved_b.append(xb)
            if rest:
                downs.append(to_next_row(xb))
        xs.append(solved)
        results = solved
        if rest:
            dtype = F32 if final else BF16
            far = [to_far_row(whole, tick, d) for d in range(2, count - tick)]
            carried = [before] if tick else []
            outs, rhs = [], []
            for c in range(CHUNKS):
                out = call(
                    lambda *a: near_kernel(tick, c, *a),
                    [shape((part, tile), dtype)], (downs[c], grad, turned, *carried),
                    [VM] * (3 + len(carried)), (), flops,
                )[0]
                outs.append(out)
                if not final:
                    rhs.append(to_next_col(out))
            if final:
                r, z, _ = place()
                results = [jnp.where(r == z, a, b) for a, b in zip(solved, outs)]
                carried = carried + [grad]
            if far:
                if not final:
                    grad = far_to_next_col(grad, tick)
                out = call(
                    lambda *a: far_kernel(tick, final, *a),
                    [shape((cols, tile), dtype)], (turned, *carried, *far),
                    [VM] * (1 + len(carried) + len(far)), (), flops,
                )[0]
                if final:
                    results = [
                        jnp.where(r >= z + 2, out[c * part : (c + 1) * part], results[c])
                        for c in range(CHUNKS)
                    ]
                else:
                    before = far_to_next_col(out, tick)
        if tick == ticks - 2:
            given = [x for solved in xs for x in solved]
            parts = call(
                lambda *a: early_kernel(count, CHUNKS, *a),
                [shape((ticks - 1, rows, width), BF16)] * count, given,
                [VM] * len(given), scratch,
            )
            sent_early = [parts[0]]
            sent_early += [from_diagonal(parts[k], k) for k in range(1, count)]
    given, more = list(results), []
    if not rest:
        given += [rhs[-1], own_tile, other_tile]
        more = [pltpu.VMEM((part, tile), F32)]
    parts = call(
        lambda *a: last_kernel(count, ticks, len(results), not rest, *a),
        [shape((rows, width), BF16)] * count, given, [VM] * len(given), scratch + more, flops,
    )
    sent = [parts[0]] + [from_last(parts[k], k) for k in range(1, count)]
    mine = call(
        lambda *a: pick_early_kernel(count, *a),
        [shape((ticks - 1, rows, width), BF16)], sent_early, [VM] * len(sent_early),
    )[0]
    theirs = cores(mine)
    early, where = call(
        lambda *a: put_early_kernel(count, ticks, *a),
        [shape(gradient.shape, F32), shape((count, 8, 128), F32)],
        (starts, gradient, mine, theirs), [SM, VM, VM, VM],
    )
    mine = call(
        lambda *a: pick_last_kernel(count, ticks, *a),
        [shape((count - ticks + 1, rows, width), BF16)], sent, [VM] * count,
    )[0]
    theirs = cores(mine)
    hbm = pl.BlockSpec(memory_space=pltpu.HBM)
    return call(
        lambda *a: put_last_kernel(count, ticks, *a),
        [shape(gradient.shape, F32)], (where, early, mine, theirs), [VM, hbm, VM, VM],
        [pltpu.VMEM((rows, width), F32), pltpu.SemaphoreType.DMA], 0, hbm, {1: 0},
    )[0]


def solution(mesh):
    in_specs = (P("row", "col"), P(("row", "col"), None), P())
    out_specs = P(("row", "col"), None)

    return jax.shard_map(body, mesh=mesh, in_specs=in_specs, out_specs=out_specs, check_vma=False)
```

```python
import jax
import jax.numpy as jnp
from jax import lax
from jax.experimental import pallas as pl
from jax.experimental.pallas import tpu as pltpu
from jax.sharding import PartitionSpec as P


TICKS = 6
CHUNKS = 2
F32 = jnp.float32
BF16 = jnp.bfloat16
VM = pl.BlockSpec(memory_space=pltpu.VMEM)
SM = pl.BlockSpec(memory_space=pltpu.SMEM)


def call(kernel, outs, args, specs, scratch=(), flops=0, out_spec=VM, aliases=()):
    n_bytes = sum(o.size * o.dtype.itemsize for o in outs)
    return pl.pallas_call(
        kernel,
        out_shape=outs,
        in_specs=specs,
        out_specs=[out_spec] * len(outs),
        input_output_aliases=dict(aliases),
        scratch_shapes=list(scratch),
        compiler_params=pltpu.CompilerParams(vmem_limit_bytes=24 << 20),
        cost_estimate=pl.CostEstimate(flops=flops, bytes_accessed=n_bytes, transcendentals=0),
    )(*args)


def shape(dims, dtype):
    return jax.ShapeDtypeStruct(dims, dtype)


def place():
    col = lax.axis_index("col")
    return lax.axis_index("row"), col // 2, col % 2


def panel_at(starts_ref, count, slot):
    found = jnp.int32(0)
    for p in range(count):
        found = jnp.where(starts_ref[p] == slot, jnp.int32(p), found)
    return found


def prep_kernel(width, grad_ref, out_ref):
    for panel in range(out_ref.shape[0]):
        out_ref[panel] = grad_ref[:, panel * width : (panel + 1) * width].astype(out_ref.dtype)


def pack_kernel(count, width, starts_ref, mine_ref, other_ref, *out_refs):
    _, z, h = place()
    lanes = lax.broadcasted_iota(jnp.int32, mine_ref.shape[1:], 1)
    low = lanes < width // 2
    for k in range(count):
        panel = panel_at(starts_ref, count, z ^ k)
        mine = mine_ref[panel].astype(F32)
        other = pltpu.roll(other_ref[panel].astype(F32), width // 2, 1)
        first = jnp.where(h == 0, mine, other)
        second = jnp.where(h == 0, other, mine)
        out_refs[k][...] = jnp.where(low, first, second).astype(out_refs[k].dtype)


def solve(rhs, own_ref, other_ref, x_ref, xb_ref):
    half = own_ref.shape[1]
    for side, tile_ref in ((slice(0, half), own_ref), (slice(half, 2 * half), other_ref)):
        value = jnp.dot(rhs, tile_ref[...], preferred_element_type=F32)
        x_ref[:, side] = value
        if xb_ref is not None:
            xb_ref[:, side] = value.astype(BF16)


def load_kernel(tile_ref, _, out_ref, sem):
    copy = pltpu.make_async_copy(tile_ref, out_ref, sem)
    copy.start()
    copy.wait()


def first_kernel(count, *refs):
    pieces = refs[:count]
    own_ref, other_ref, x_ref, xb_ref, grad_ref, natural = refs[count:]
    r, z, _ = place()
    rows, width = pieces[0].shape
    for k in range(count):
        source = z ^ k
        piece = pieces[k][...].astype(F32)
        top = pl.multiple_of(source * (2 * rows), 8)
        natural[pl.ds(top, rows), :] = piece
        natural[pl.ds(pl.multiple_of(top + rows, 8), rows), :] = pltpu.roll(piece, width // 2, 1)
    grad_ref[...] = jnp.transpose(natural[...])[: width // 2].astype(BF16)

    @pl.when(r == z)
    def _():
        solve(grad_ref[: x_ref.shape[0]], own_ref, other_ref, x_ref, xb_ref)


def solve_kernel(tick, top, n_before, rhs_ref, own_ref, other_ref, *refs):
    r, z, _ = place()
    before, outs = refs[:n_before], refs[n_before:]
    x_ref, xb_ref = outs[0], outs[1] if len(outs) > 1 else None
    rows = x_ref.shape[0]

    @pl.when((r == z) & (z >= tick))
    def _():
        solve(rhs_ref[top : top + rows], own_ref, other_ref, x_ref, xb_ref)
        if len(outs) > 2:
            for c, ref in enumerate(before):
                outs[2][c * rows : (c + 1) * rows] = ref[...]
            outs[2][n_before * rows :] = xb_ref[...]


def turn_kernel(own_ref, other_ref, _, out_ref):
    r, z, _ = place()
    half = own_ref.shape[1]

    @pl.when(r > z)
    def _():
        out_ref[:half] = jnp.transpose(own_ref[...])
        out_ref[half:] = jnp.transpose(other_ref[...])


def near_kernel(tick, c, x_ref, grad_ref, turned_ref, *refs):
    out_ref = refs[-1]
    rows = out_ref.shape[0]
    mine = slice(c * rows, (c + 1) * rows)
    r, z, _ = place()

    @pl.when((r == z + 1) & (z >= tick))
    def _():
        value = grad_ref[mine].astype(F32)
        if tick:
            value = value - refs[0][mine].astype(F32)
        value = value - jnp.dot(x_ref[...], turned_ref[...], preferred_element_type=F32)
        out_ref[...] = value.astype(out_ref.dtype)


def far_kernel(tick, final, turned_ref, *refs):
    out_ref = refs[-1]
    before = refs[0] if tick else None
    grad_ref = refs[1] if final else None
    x_refs = refs[(1 if tick else 0) + (1 if final else 0) : -1]
    r, z, _ = place()
    for i, x_ref in enumerate(x_refs):

        @pl.when((r == z + 2 + i) & (z >= tick))
        def _():
            value = jnp.dot(x_ref[...], turned_ref[...], preferred_element_type=F32)
            if before is not None:
                value = value + before[...].astype(F32)
            if grad_ref is not None:
                value = grad_ref[...].astype(F32) - value
            out_ref[...] = value.astype(out_ref.dtype)


def fold(x_refs, natural):
    _, _, h = place()
    half, width = x_refs[0].shape[1] // 2, natural.shape[1]
    own = jnp.concatenate([ref[:, :half] for ref in x_refs], axis=0)
    other = jnp.concatenate([ref[:, half:] for ref in x_refs], axis=0)
    top = pl.multiple_of(h * half, 8)
    natural[pl.ds(top, half), : width // 2] = jnp.transpose(own)
    natural[pl.ds(pl.multiple_of(half - top, 8), half), : width // 2] = jnp.transpose(other)


def folded(natural, rows, target):
    width = natural.shape[1]
    lanes = lax.broadcasted_iota(jnp.int32, (rows, width), 1)
    top = pl.multiple_of(target * (2 * rows), 8)
    upper = natural[pl.ds(top, rows), :]
    lower = natural[pl.ds(pl.multiple_of(top + rows, 8), rows), :]
    return jnp.where(lanes < width // 2, upper, pltpu.roll(lower, width // 2, 1))


def early_kernel(count, n_chunks, *refs):
    x_refs, out_refs, natural = refs[: -count - 1], refs[-count - 1 : -1], refs[-1]
    r, z, _ = place()
    rows = out_refs[0].shape[1]

    @pl.when(r == z)
    def _():
        for t in range(len(x_refs) // n_chunks):
            fold(x_refs[t * n_chunks : (t + 1) * n_chunks], natural)
            for k in range(count):
                out_refs[k][t] = folded(natural, rows, z ^ k).astype(out_refs[k].dtype)


def last_kernel(count, ticks, n_before, solves, *refs):
    before, refs = refs[:n_before], refs[n_before:]
    r, z, _ = place()
    if solves:
        rhs_ref, own_ref, other_ref = refs[:3]
        out_refs, natural, x_ref = refs[3:-2], refs[-2], refs[-1]
    else:
        out_refs, natural = refs[:-1], refs[-1]
    rows = out_refs[0].shape[0]

    @pl.when((z >= ticks - 1) & (z <= r))
    def _():
        x_refs = list(before)
        if solves:
            solve(rhs_ref[...], own_ref, other_ref, x_ref, None)
            x_refs.append(x_ref)
        fold(x_refs, natural)
        for k in range(count):
            out_refs[k][...] = folded(natural, rows, z ^ k).astype(out_refs[k].dtype)


def pick_early_kernel(count, *refs):
    out_ref = refs[-1]
    r, z, _ = place()
    for k in range(count):

        @pl.when((z ^ r) == k)
        def _():
            out_ref[...] = refs[k][...]


def pick_last_kernel(count, ticks, *refs):
    out_ref = refs[-1]
    r, z, _ = place()
    for k in range(count):
        source = z ^ k

        @pl.when((source >= ticks - 1) & (source <= r))
        def _():
            out_ref[source - (ticks - 1)] = refs[k][...]


def join(mine, other, h):
    width = mine.shape[1]
    lanes = lax.broadcasted_iota(jnp.int32, mine.shape, 1)
    other = pltpu.roll(other.astype(F32), width // 2, 1)
    mine = mine.astype(F32)
    low = jnp.where(h == 0, mine, other)
    high = jnp.where(h == 0, other, mine)
    return jnp.where(lanes < width // 2, low, high)


def put_early_kernel(count, ticks, starts_ref, grad_ref, mine_ref, other_ref, out_ref, where_ref):
    r, _, h = place()
    width = mine_ref.shape[2]
    for s in range(count):
        panel = panel_at(starts_ref, count, s)
        where_ref[s] = jnp.full(where_ref.shape[1:], panel.astype(F32))
        begin = pl.multiple_of(panel * width, width)

        @pl.when(r < s)
        def _():
            out_ref[:, pl.ds(begin, width)] = grad_ref[:, pl.ds(begin, width)]

        @pl.when((r >= s) & (r - s <= ticks - 2))
        def _():
            t = r - s
            out_ref[:, pl.ds(begin, width)] = join(mine_ref[t], other_ref[t], h)


def put_last_kernel(count, ticks, where_ref, _, mine_ref, other_ref, out_ref, joined, sem):
    r, _, h = place()
    width = mine_ref.shape[2]
    for s in range(count - ticks + 1):

        @pl.when(r - s >= ticks - 1)
        def _():
            panel = jnp.max(where_ref[s]).astype(jnp.int32)
            begin = pl.multiple_of(panel * width, width)
            joined[...] = join(mine_ref[s], other_ref[s], h)
            copy = pltpu.make_async_copy(joined, out_ref.at[:, pl.ds(begin, width)], sem)
            copy.start()
            copy.wait()


def body(factor, gradient, starts):
    count = starts.shape[0]
    ticks = min(TICKS, count)
    rows = gradient.shape[0]
    width = gradient.shape[1] // count
    tile, _ = factor.shape
    cols = width // 2
    devices = [(r, z, h) for r in range(count) for z in range(count) for h in range(2)]

    def move(array, target):
        pairs = []
        for r, z, h in devices:
            goal = target(r, z, h)
            if goal is not None:
                pairs.append(((r * count + z) * 2 + h, (goal[0] * count + goal[1]) * 2 + goal[2]))
        return lax.ppermute(array, ("row", "col"), pairs)

    def cores(array):
        return move(array, lambda r, z, h: (r, z, 1 - h))

    def along(array, k):
        return move(array, lambda r, z, h: (r, z ^ k, h))

    def from_diagonal(array, k):
        return move(array, lambda r, z, h: (r, z ^ k, h) if r == z else None)

    def to_far_row(array, tick, d):
        def target(r, z, h):
            return (r + d, z, h) if r == z and z >= tick and r + d < count else None

        return move(array, target)

    def to_next_row(array):
        def target(r, z, h):
            idle, far = range(z - 1, -1, -1), range(count - 1, z + 1, -1)
            cycle = [z] + [z + 1] * (z + 1 < count) + [*far] + [*idle]
            return cycle[(cycle.index(r) + 1) % count], z, h

        return move(array, target)

    def to_next_col(array):
        def target(r, z, h):
            base = z - z % 2 if r % 2 else z - 1 + z % 2
            if base < 0 or base + 1 >= count:
                return r ^ 2, z, h
            lead = (r ^ 2) == base + 1 or (r != base + 1 and r & 2)
            if (z == base) == (not lead):
                return r, base + 1 if z == base else base, h
            return r ^ 2, z, h

        return move(array, target)

    def from_last(array, k):
        def target(r, z, h):
            return (r, z ^ k, h) if ticks - 1 <= z <= r else None

        return move(array, target)

    def far_to_next_col(array, tick):
        def target(r, z, h):
            return (r, z + 1, h) if r >= z + 2 and z >= tick else None

        return move(array, target)

    flops = 2 * cols * tile * tile
    mine = call(
        lambda *a: prep_kernel(width, *a),
        [shape((count, rows, width), BF16)], (gradient,), [VM],
    )[0]
    theirs = cores(mine)
    pieces = call(
        lambda *a: pack_kernel(count, width, *a),
        [shape((rows, width), BF16)] * count, (starts, mine, theirs), [SM, VM, VM],
    )
    arrived = [pieces[0]] + [along(pieces[k], k) for k in range(1, count)]
    other_tile = cores(factor)
    own_tile = call(
        load_kernel, [shape(factor.shape, BF16)], (factor, pieces[0]),
        [pl.BlockSpec(memory_space=pl.ANY), VM], [pltpu.SemaphoreType.DMA],
    )[0]
    part = cols // CHUNKS
    pair = [shape((part, tile), F32), shape((part, tile), BF16)]
    scratch = [pltpu.VMEM((tile, width), F32)]
    x, xb, grad = call(
        lambda *a: first_kernel(count, *a),
        pair + [shape((cols, tile), BF16)], (*arrived, own_tile, other_tile), [VM] * (count + 2),
        scratch, flops,
    )
    turned = call(
        turn_kernel, [shape((tile, tile), BF16)], (own_tile, other_tile, pieces[0]), [VM] * 3,
    )[0]
    xs, before, sent_early = [], None, []
    for tick in range(ticks):
        final = tick == ticks - 1
        rest = count - 1 > tick
        solved, solved_b, downs = [], [], []
        for c in range(CHUNKS):
            if tick or c:
                if final and not rest and c == CHUNKS - 1:
                    break
                source, top = (rhs[c], 0) if tick else (grad, c * part)
                joins = c == CHUNKS - 1 and CHUNKS > 1 and count - 2 > tick
                outs = pair + ([shape((cols, tile), BF16)] if joins else [])
                outs = outs if rest else outs[:1]
                given = solved_b if joins else []
                done = call(
                    lambda *a: solve_kernel(tick, top, len(given), *a),
                    outs, (source, own_tile, other_tile, *given), [VM] * (3 + len(given)), (), flops,
                )
                x, xb, whole = done[0], done[1 % len(done)], done[-1]
            else:
                whole = xb
            solved.append(x)
            solved_b.append(xb)
            if rest:
                downs.append(to_next_row(xb))
        xs.append(solved)
        results = solved
        if rest:
            dtype = F32 if final else BF16
            far = [to_far_row(whole, tick, d) for d in range(2, count - tick)]
            carried = [before] if tick else []
            outs, rhs = [], []
            for c in range(CHUNKS):
                out = call(
                    lambda *a: near_kernel(tick, c, *a),
                    [shape((part, tile), dtype)], (downs[c], grad, turned, *carried),
                    [VM] * (3 + len(carried)), (), flops,
                )[0]
                outs.append(out)
                if not final:
                    rhs.append(to_next_col(out))
            if final:
                r, z, _ = place()
                results = [jnp.where(r == z, a, b) for a, b in zip(solved, outs)]
                carried = carried + [grad]
            if far:
                if not final:
                    grad = far_to_next_col(grad, tick)
                out = call(
                    lambda *a: far_kernel(tick, final, *a),
                    [shape((cols, tile), dtype)], (turned, *carried, *far),
                    [VM] * (1 + len(carried) + len(far)), (), flops,
                )[0]
                if final:
                    results = [
                        jnp.where(r >= z + 2, out[c * part : (c + 1) * part], results[c])
                        for c in range(CHUNKS)
                    ]
                else:
                    before = far_to_next_col(out, tick)
        if tick == ticks - 2:
            given = [x for solved in xs for x in solved]
            parts = call(
                lambda *a: early_kernel(count, CHUNKS, *a),
                [shape((ticks - 1, rows, width), BF16)] * count, given,
                [VM] * len(given), scratch,
            )
            sent_early = [parts[0]]
            sent_early += [from_diagonal(parts[k], k) for k in range(1, count)]
    given, more = list(results), []
    if not rest:
        given += [rhs[-1], own_tile, other_tile]
        more = [pltpu.VMEM((part, tile), F32)]
    parts = call(
        lambda *a: last_kernel(count, ticks, len(results), not rest, *a),
        [shape((rows, width), BF16)] * count, given, [VM] * len(given), scratch + more, flops,
    )
    sent = [parts[0]] + [from_last(parts[k], k) for k in range(1, count)]
    mine = call(
        lambda *a: pick_early_kernel(count, *a),
        [shape((ticks - 1, rows, width), BF16)], sent_early, [VM] * len(sent_early),
    )[0]
    theirs = cores(mine)
    early, where = call(
        lambda *a: put_early_kernel(count, ticks, *a),
        [shape(gradient.shape, F32), shape((count, 8, 128), F32)],
        (starts, gradient, mine, theirs), [SM, VM, VM, VM],
    )
    mine = call(
        lambda *a: pick_last_kernel(count, ticks, *a),
        [shape((count - ticks + 1, rows, width), BF16)], sent, [VM] * count,
    )[0]
    theirs = cores(mine)
    hbm = pl.BlockSpec(memory_space=pltpu.HBM)
    return call(
        lambda *a: put_last_kernel(count, ticks, *a),
        [shape(gradient.shape, F32)], (where, early, mine, theirs), [VM, hbm, VM, VM],
        [pltpu.VMEM((rows, width), F32), pltpu.SemaphoreType.DMA], 0, hbm, {1: 0},
    )[0]


def solution(mesh):
    in_specs = (P("row", "col"), P(("row", "col"), None), P())
    out_specs = P(("row", "col"), None)

    return jax.shard_map(body, mesh=mesh, in_specs=in_specs, out_specs=out_specs, check_vma=False)
```
